32 devices in a mesh: dp: 2 (over y), expert: 16 (over z, x, core).
Axes of the slice: x: 2, y: 2, z: 4, core: 2. Of those that a mesh axis runs over, the one named last changes fastest.
Arguments:
- tokens: bfloat16 [2048, 3584], P('expert', 'dp'), may hold values from -6 to 6
- expert_ids: int32 [2048, 8], P('expert'), may hold values from 0 to 63, all different within a row; in each aligned block of 128 rows (0 to 127, 128 to 255, ...) at most 32 rows name the same one
- gate_weight: float32 [2048, 8], P('expert'), may hold values from 0.1 to 0.6
- w_gate: bfloat16 [16, 3584, 1024], P('expert', 'dp'), may hold values from -0.09375 to 0.09375
- w_up: bfloat16 [16, 3584, 1024], P('expert', 'dp'), may hold values from -0.09375 to 0.09375
- w_down: bfloat16 [16, 1024, 3584], P('expert', None, 'dp'), may hold values from -0.1875 to 0.1875
- grad_out: bfloat16 [2048, 3584], P('expert', 'dp'), may hold values from -6 to 6
Outputs:
- output: bfloat16 [2048, 3584], P('expert', 'dp')
- grad_tokens: bfloat16 [2048, 3584], P('expert', 'dp')
- grad_down: bfloat16 [16, 1024, 3584], P('expert', None, 'dp')
The draws below stay inside these ranges and needn't reach their ends.
Inputs may be any that keep to these rules, and one draw needn't show every extreme that they name: `expert_ids`: each row names 8 different experts. Among the rows of one device no expert is named by more than 32 rows, and in some device's rows some expert is named by exactly 32 rows.
All inputs are finite; a program needn't handle non-finite values.
Results may differ from the reference program's by a relative error of at most 0.024.
Values may be sent and summed in bfloat16 or wider, within the bound.
A program may use at most 64 MiB of HBM per device.

```python
import math
import jax
import jax.numpy as jnp
import numpy as np
from jax import lax

D = 3584
HID = 1024
TOP = 8
TOK_DEV = 128
EXPERTS = 16
ALL_EXPERTS = 64
CAP = 32
TOKENS = 2048
N_DP = 2
N_EXPERT = 16


def steps_of(own_key, shape, shards, least, high):
    loudness, own = 1.0, jax.random.fold_in(own_key, 6)
    for dim, blocks in shards:
        steps = jnp.exp(jax.random.uniform(jax.random.fold_in(own, dim), (blocks,), jnp.float32, least / len(shards), high / len(shards)))
        loudness = loudness * jnp.repeat(steps, shape[dim] // blocks).reshape([-1 if axis == dim else 1 for axis in range(len(shape))])
    return loudness


def assign_block(key, own, number, rows, amount, top, bound, skew):
    order = jax.random.permutation(key, amount)
    packed, common = portions_of(amount, rows * top, bound, skew, True), portions_of(amount, rows * top, bound, skew, False)
    places = jnp.arange(amount)

    def named(tallies, rotation):
        used = int((tallies > 0).sum())
        fixed = max(1, used // 4)
        shifted = fixed + (places - fixed + rotation * (used - fixed)) % max(1, amount - fixed)
        return jnp.zeros((amount,), jnp.int32).at[order[jnp.where(places < fixed, places, shifted)]].set(jnp.asarray(tallies, jnp.int32))

    tallies = jnp.where(number % 4 == 0, named(packed, number // 4), named(common, number - number // 4 - 1))
    mixed = jax.random.permutation(jax.random.fold_in(own, 3), amount)
    giver, taker = mixed[0:amount // 2 * 2:2], mixed[1:amount // 2 * 2:2]
    slack = jnp.minimum(tallies[giver] - 1, bound - tallies[taker]) // 2
    slack = jnp.where((giver == order[0]) | (taker == order[0]) | (tallies[taker] == 0), 0, jnp.maximum(slack, 0))
    shifted = jax.random.randint(jax.random.fold_in(own, 4), (amount // 2,), 0, 1 << 20) % (slack + 1)
    tallies = tallies.at[giver].add(-shifted).at[taker].add(shifted)
    members = jnp.searchsorted(jnp.cumsum(tallies), jnp.arange(rows * top), side="right").astype(jnp.int32)
    listing = members.reshape(top, rows).T
    listing = listing[jax.random.permutation(jax.random.fold_in(own, 1), rows)]
    rotation = jax.random.randint(jax.random.fold_in(own, 2), (rows, 1), 0, top)
    return jnp.take_along_axis(listing, (jnp.arange(top)[None, :] + rotation) % top, axis=1)


def portions_of(count, total, most, slope, full):
    loads = [(1 << 20) // math.isqrt(grade ** slope) + 1 for grade in range(1, count + 1)]
    largest = most if full else min(most, max(-(-total // count), total * loads[0] // sum(loads)))
    least = 1 if total - largest >= count - 1 else 0
    given, spare = [largest] + [least] * (count - 1), total - largest - least * (count - 1)
    while spare > 0:
        movable = [i for i in range(1, count) if given[i] < largest] or [i for i in range(1, count) if given[i] < most]
        whole, budget = sum([loads[i] for i in movable]), spare
        for i in movable:
            extra = min(most - given[i], max(1, budget * loads[i] // whole), spare)
            given[i] = given[i] + extra
            spare = spare - extra
    return np.array(given)


def noise(rng, dims, scale, limit, split=(), kind=jnp.bfloat16):
    array = jax.random.normal(rng, dims, jnp.float32) * scale
    if len(split) > 0:
        array = steps_of(rng, dims, split, -0.22, 0.18) * array
    return jnp.clip(array, min=-limit, max=limit).astype(kind)


def setup_inputs(seed: int = 0) -> dict:
    key_of = jax.random.split(jax.random.key(seed), 8)
    tokens = noise(key_of[0], (TOKENS, D), 1.0, 6.0, ((0, 16), (1, 2)))
    expert_ids_keys = jax.random.split(jax.random.fold_in(key_of[1], 1), TOKENS // TOK_DEV)
    expert_ids_turns = jax.random.permutation(jax.random.fold_in(key_of[1], 3), TOKENS // TOK_DEV)
    expert_ids = jax.vmap(lambda own, number: assign_block(jax.random.fold_in(key_of[1], 2), own, number, TOK_DEV, ALL_EXPERTS, TOP, CAP, 2))(expert_ids_keys, expert_ids_turns).reshape((TOKENS, TOP))
    gate_weight = jnp.clip(0.1 + 0.5 * jax.random.uniform(key_of[2], (TOKENS, TOP), jnp.float32) ** steps_of(key_of[2], (TOKENS, TOP), ((0, 16),), -0.2, 0.2), 0.1, 0.6)
    w_gate = noise(key_of[3], (EXPERTS, D, HID), D ** -0.5, 0.09375, ((0, 16), (1, 2)))
    w_up = noise(key_of[4], (EXPERTS, D, HID), D ** -0.5, 0.09375, ((0, 16), (1, 2)))
    w_down = noise(key_of[5], (EXPERTS, HID, D), HID ** -0.5, 0.1875, ((0, 16), (2, 2)))
    grad_out = noise(key_of[6], (TOKENS, D), 1.0, 6.0, ((0, 16), (1, 2)))
    return dict(tokens=tokens, expert_ids=expert_ids, gate_weight=gate_weight, w_gate=w_gate, w_up=w_up, w_down=w_down, grad_out=grad_out)


def slots_of(block_ids):
    hot = (block_ids[:, None] == jnp.arange(EXPERTS, dtype=jnp.int32)[None, :]).astype(jnp.int32)
    before = jnp.cumsum(hot, axis=0) - hot
    return jnp.sum(before * hot, axis=1).astype(jnp.int32)


def sliced_product(left, right):
    step_cols = D // N_DP
    total = None
    for index in range(N_DP):
        part = jnp.dot(left[:, index * step_cols:(index + 1) * step_cols], right[index * step_cols:(index + 1) * step_cols], preferred_element_type=jnp.float32)
        part = lax.optimization_barrier(part.astype(jnp.bfloat16)).astype(jnp.float32)
        total = part if total is None else total + part
    return total


def expert_pass(operands):
    x_rows, c_rows, gate_mat, up_mat, down_mat = operands
    gate_pre = sliced_product(x_rows, gate_mat)
    up_pre = sliced_product(x_rows, up_mat)
    hidden = (jax.nn.silu(gate_pre) * up_pre).astype(jnp.bfloat16)
    expert_out = jnp.dot(hidden, down_mat, preferred_element_type=jnp.float32).astype(jnp.bfloat16)
    grad_hidden = sliced_product(c_rows, down_mat.T)
    sig = jax.nn.sigmoid(gate_pre)
    grad_gate = (grad_hidden * up_pre * sig * (1.0 + gate_pre * (1.0 - sig))).astype(jnp.bfloat16)
    grad_up = (grad_hidden * jax.nn.silu(gate_pre)).astype(jnp.bfloat16)
    grad_rows = (jnp.dot(grad_gate, gate_mat.T, preferred_element_type=jnp.float32) + jnp.dot(grad_up, up_mat.T, preferred_element_type=jnp.float32)).astype(jnp.bfloat16)
    grad_down = jnp.dot(hidden.T, c_rows, preferred_element_type=jnp.float32).astype(jnp.bfloat16)
    return expert_out, grad_rows, grad_down


def reference(tokens, expert_ids, gate_weight, w_gate, w_up, w_down, grad_out):
    pair_total = TOKENS * TOP
    block_ids = expert_ids.reshape(N_EXPERT, TOK_DEV * TOP)
    slot_index = jax.vmap(slots_of)(block_ids).reshape(pair_total)
    flat_ids = expert_ids.reshape(pair_total).astype(jnp.int32)
    in_window = flat_ids < EXPERTS
    safe_ids = jnp.where(in_window, flat_ids, 0).astype(jnp.int32)
    used = in_window.astype(jnp.float32)[:, None]
    pair_iota = jnp.arange(pair_total, dtype=jnp.int32)
    source_block = pair_iota // (TOK_DEV * TOP)
    row_index = (source_block * CAP + slot_index).astype(jnp.int32)
    token_index = (pair_iota // TOP).astype(jnp.int32)
    token_rows = tokens[token_index]
    scaled = (gate_weight.reshape(pair_total)[:, None] * grad_out[token_index].astype(jnp.float32)).astype(jnp.bfloat16)
    buffer_rows = N_EXPERT * CAP
    scatter_ids = jnp.where(in_window, flat_ids, EXPERTS).astype(jnp.int32)
    x_buf = jnp.zeros((EXPERTS, buffer_rows, D), jnp.bfloat16).at[scatter_ids, row_index].set(token_rows, mode="drop")
    c_buf = jnp.zeros((EXPERTS, buffer_rows, D), jnp.bfloat16).at[scatter_ids, row_index].set(scaled, mode="drop")
    expert_out, grad_rows, grad_down = lax.map(expert_pass, (x_buf, c_buf, w_gate, w_up, w_down))
    out_pairs = expert_out[safe_ids, row_index].astype(jnp.float32) * used
    weighted = gate_weight.reshape(pair_total)[:, None] * out_pairs
    output = jnp.sum(weighted.reshape(TOKENS, TOP, D), axis=1).astype(jnp.bfloat16)
    grad_pairs = grad_rows[safe_ids, row_index].astype(jnp.float32) * used
    grad_tokens = jnp.sum(grad_pairs.reshape(TOKENS, TOP, D), axis=1).astype(jnp.bfloat16)
    return output, grad_tokens, grad_down
```

```python
import jax
import jax.numpy as jnp
from jax import lax
from jax.sharding import PartitionSpec as P


def dp_sum(part):
    count = lax.axis_size("dp")
    part = part.astype(jnp.bfloat16)
    total = part.astype(jnp.float32)
    for shift in range(1, count):
        moved = lax.ppermute(part, "dp", [(i, (i + shift) % count) for i in range(count)])
        total = total + moved.astype(jnp.float32)
    return total


def local(tokens, expert_ids, gate_weight, w_gate, w_up, w_down, grad_out):
    tok_dev, fanout = expert_ids.shape
    feature_cols = tokens.shape[1]
    experts = lax.axis_size("expert")
    capacity = max(2, min(tok_dev, 2 * tok_dev * fanout // (4 * experts)))
    ids = jnp.arange(experts, dtype=jnp.int32)
    named = expert_ids[None, :, :] == ids[:, None, None]
    hot = jnp.any(named, axis=2)
    gate_of = jnp.sum(jnp.where(named, gate_weight[None, :, :], 0.0), axis=2)
    rows = jnp.arange(tok_dev, dtype=jnp.int32)
    earlier = (rows[:, None] < rows[None, :]).astype(jnp.bfloat16)
    before = jnp.dot(hot.astype(jnp.bfloat16), earlier, preferred_element_type=jnp.float32)
    slot_of = jnp.where(hot, before.astype(jnp.int32), -1)
    placing = slot_of[:, None, :] == jnp.arange(capacity, dtype=jnp.int32)[None, :, None]
    select = placing.astype(jnp.bfloat16).reshape(experts * capacity, tok_dev)
    slot_gate = jnp.sum(jnp.where(placing, gate_of[:, None, :], 0.0), axis=2).reshape(experts * capacity)
    x_slab = jnp.dot(select, tokens, preferred_element_type=jnp.float32).astype(jnp.bfloat16)
    x_slab = x_slab.reshape(experts, capacity, feature_cols)
    cot_rows = jnp.dot(select, grad_out, preferred_element_type=jnp.float32)
    c_slab = (slot_gate[:, None] * cot_rows).astype(jnp.bfloat16)
    c_slab = c_slab.reshape(experts, capacity, feature_cols)
    gate_mat = w_gate[0]
    up_mat = w_up[0]
    down_mat = w_down[0]
    row_total = experts * capacity
    transposed = (((1,), (1,)), ((), ()))
    arrived = lax.all_to_all(x_slab, "expert", split_axis=0, concat_axis=0, tiled=True)
    x_rows = arrived.reshape(row_total, feature_cols)
    gate_part = jnp.dot(x_rows, gate_mat, preferred_element_type=jnp.float32)
    up_part = jnp.dot(x_rows, up_mat, preferred_element_type=jnp.float32)
    gate_pre = dp_sum(gate_part)
    up_pre = dp_sum(up_part)
    hidden = (jax.nn.silu(gate_pre) * up_pre).astype(jnp.bfloat16)
    out_rows = jnp.dot(hidden, down_mat, preferred_element_type=jnp.float32).astype(jnp.bfloat16)
    gate_pre, up_pre, hidden, out_rows = (
        gate_pre,
        up_pre,
        hidden,
        out_rows.reshape(experts, capacity, feature_cols),
    )
    back_out = lax.all_to_all(out_rows, "expert", split_axis=0, concat_axis=0, tiled=True)
    arrived_grads = lax.all_to_all(c_slab, "expert", split_axis=0, concat_axis=0, tiled=True)
    c_rows = arrived_grads.reshape(row_total, feature_cols)
    hidden_part = lax.dot_general(c_rows, down_mat, transposed, preferred_element_type=jnp.float32)
    sig = jax.nn.sigmoid(gate_pre)
    grad_hidden = dp_sum(hidden_part)
    grad_gate = (grad_hidden * up_pre * sig * (1.0 + gate_pre * (1.0 - sig))).astype(jnp.bfloat16)
    grad_up = (grad_hidden * jax.nn.silu(gate_pre)).astype(jnp.bfloat16)
    grad_rows = lax.dot_general(grad_gate, gate_mat, transposed, preferred_element_type=jnp.float32)
    grad_rows = grad_rows + lax.dot_general(
        grad_up, up_mat, transposed, preferred_element_type=jnp.float32
    )
    grad_rows = grad_rows.astype(jnp.bfloat16).reshape(experts, capacity, feature_cols)
    down_grad = lax.dot_general(
        hidden, c_rows, (((0,), (0,)), ((), ())), preferred_element_type=jnp.float32
    )
    grad_rows, down_grad = (grad_rows, down_grad.astype(jnp.bfloat16))
    back_grads = lax.all_to_all(grad_rows, "expert", split_axis=0, concat_axis=0, tiled=True)
    scaled = back_out.reshape(row_total, feature_cols).astype(jnp.float32) * slot_gate[:, None]
    output = jnp.dot(select.T, scaled.astype(jnp.bfloat16), preferred_element_type=jnp.float32)
    output = output.astype(jnp.bfloat16)
    grad_flat = back_grads.reshape(row_total, feature_cols)
    grad_tokens = jnp.dot(select.T, grad_flat, preferred_element_type=jnp.float32).astype(
        jnp.bfloat16
    )
    return (output, grad_tokens, down_grad.reshape(1, down_grad.shape[0], feature_cols))


def solution(mesh):
    return jax.shard_map(
        local,
        mesh=mesh,
        in_specs=(
            P("expert", "dp"),
            P("expert", None),
            P("expert", None),
            P("expert", "dp", None),
            P("expert", "dp", None),
            P("expert", None, "dp"),
            P("expert", "dp"),
        ),
        out_specs=(P("expert", "dp"), P("expert", "dp"), P("expert", None, "dp")),
        check_vma=False,
    )
```

```python
import jax
import jax.numpy as jnp
from jax import lax
from jax.sharding import PartitionSpec as P


def dp_sum(part):
    count = lax.axis_size("dp")
    part = part.astype(jnp.bfloat16)
    total = part.astype(jnp.float32)
    for shift in range(1, count):
        moved = lax.ppermute(part, "dp", [(i, (i + shift) % count) for i in range(count)])
        total = total + moved.astype(jnp.float32)
    return total


def exchange(rows, after=None):
    if after is not None:
        rows, _ = lax.optimization_barrier((rows, after))
    return lax.all_to_all(rows, "expert", split_axis=0, concat_axis=0, tiled=True)


def local(tokens, expert_ids, gate_weight, w_gate, w_up, w_down, grad_out):
    tok_dev, fanout = expert_ids.shape
    feature_cols = tokens.shape[1]
    experts = lax.axis_size("expert")
    capacity = max(2, min(tok_dev, 2 * tok_dev * fanout // (4 * experts)))
    ids = jnp.arange(experts, dtype=jnp.int32)
    named = expert_ids[None, :, :] == ids[:, None, None]
    hot = jnp.any(named, axis=2)
    gate_of = jnp.sum(jnp.where(named, gate_weight[None, :, :], 0.0), axis=2)
    rows = jnp.arange(tok_dev, dtype=jnp.int32)
    earlier = (rows[:, None] < rows[None, :]).astype(jnp.bfloat16)
    before = jnp.dot(hot.astype(jnp.bfloat16), earlier, preferred_element_type=jnp.float32)
    slot_of = jnp.where(hot, before.astype(jnp.int32), -1)
    placing = slot_of[:, None, :] == jnp.arange(capacity, dtype=jnp.int32)[None, :, None]
    select = placing.astype(jnp.bfloat16).reshape(experts * capacity, tok_dev)
    slot_gate = jnp.sum(jnp.where(placing, gate_of[:, None, :], 0.0), axis=2).reshape(experts * capacity)
    row_total = experts * capacity
    transposed = (((1,), (1,)), ((), ()))
    gate_mat = w_gate[0]
    up_mat = w_up[0]
    down_mat = w_down[0]

    pieces = 2
    span = capacity // pieces
    select_slots = select.reshape(experts, capacity, tok_dev)
    arrived = None
    gate_parts, up_parts, ready = [], [], []
    for piece in range(pieces):
        chosen = select_slots[:, piece * span : (piece + 1) * span].reshape(experts * span, tok_dev)
        x_slab = jnp.dot(chosen, tokens, preferred_element_type=jnp.float32).astype(jnp.bfloat16)
        arrived = exchange(x_slab.reshape(experts, span, feature_cols), arrived)
        x_rows = arrived.reshape(experts * span, feature_cols)
        gate_part = jnp.dot(x_rows, gate_mat, preferred_element_type=jnp.float32).astype(jnp.bfloat16)
        up_part = jnp.dot(x_rows, up_mat, preferred_element_type=jnp.float32).astype(jnp.bfloat16)
        gate_parts.append(dp_sum(gate_part))
        up_parts.append(dp_sum(up_part))
        ready.append((gate_parts[-1], up_part))

    cot_rows = jnp.dot(select, grad_out, preferred_element_type=jnp.float32)
    c_slab = (slot_gate[:, None] * cot_rows).astype(jnp.bfloat16)
    c_arrived = exchange(c_slab.reshape(experts, capacity, feature_cols), (arrived, ready[0]))
    c_rows = c_arrived.reshape(row_total, feature_cols)
    hidden_part = lax.dot_general(c_rows, down_mat, transposed, preferred_element_type=jnp.float32)

    def joined(parts):
        parts = [part.reshape(experts, span, part.shape[1]) for part in parts]
        return jnp.concatenate(parts, axis=1).reshape(row_total, parts[0].shape[2])

    gate_pre, up_pre = joined(gate_parts), joined(up_parts)
    hidden = (jax.nn.silu(gate_pre) * up_pre).astype(jnp.bfloat16)
    out_rows = jnp.dot(hidden, down_mat, preferred_element_type=jnp.float32).astype(jnp.bfloat16)
    back_out = exchange(out_rows.reshape(experts, capacity, feature_cols), c_arrived)

    grad_hidden = dp_sum(hidden_part)
    sig = jax.nn.sigmoid(gate_pre)
    grad_gate = (grad_hidden * up_pre * sig * (1.0 + gate_pre * (1.0 - sig))).astype(jnp.bfloat16)
    grad_up = (grad_hidden * jax.nn.silu(gate_pre)).astype(jnp.bfloat16)
    grad_rows = lax.dot_general(grad_gate, gate_mat, transposed, preferred_element_type=jnp.float32)
    grad_rows = grad_rows + lax.dot_general(
        grad_up, up_mat, transposed, preferred_element_type=jnp.float32
    )
    grad_rows = grad_rows.astype(jnp.bfloat16).reshape(experts, capacity, feature_cols)
    back_grads = exchange(grad_rows, back_out)
    down_grad = lax.dot_general(
        hidden, c_rows, (((0,), (0,)), ((), ())), preferred_element_type=jnp.float32
    ).astype(jnp.bfloat16)

    scaled = back_out.reshape(row_total, feature_cols).astype(jnp.float32) * slot_gate[:, None]
    output = jnp.dot(select.T, scaled.astype(jnp.bfloat16), preferred_element_type=jnp.float32)
    output = output.astype(jnp.bfloat16)
    grad_flat = back_grads.reshape(row_total, feature_cols)
    grad_tokens = jnp.dot(select.T, grad_flat, preferred_element_type=jnp.float32).astype(
        jnp.bfloat16
    )
    return (output, grad_tokens, down_grad.reshape(1, down_grad.shape[0], feature_cols))


def solution(mesh):
    return jax.shard_map(
        local,
        mesh=mesh,
        in_specs=(
            P("expert", "dp"),
            P("expert", None),
            P("expert", None),
            P("expert", "dp", None),
            P("expert", "dp", None),
            P("expert", None, "dp"),
            P("expert", "dp"),
        ),
        out_specs=(P("expert", "dp"), P("expert", "dp"), P("expert", None, "dp")),
        check_vma=False,
    )
```

```python
import functools

import jax
import jax.numpy as jnp
from jax import lax
from jax.experimental import pallas as pl
from jax.experimental.pallas import tpu as pltpu
from jax.sharding import PartitionSpec as P


def dp_sum(part):
    count = lax.axis_size("dp")
    part = part.astype(jnp.bfloat16)
    total = part.astype(jnp.float32)
    for shift in range(1, count):
        moved = lax.ppermute(part, "dp", [(i, (i + shift) % count) for i in range(count)])
        total = total + moved.astype(jnp.float32)
    return total


def exchange(rows, after=None):
    if after is not None:
        rows, _ = lax.optimization_barrier((rows, after))
    return lax.all_to_all(rows, "expert", split_axis=0, concat_axis=0, tiled=True)


PIECES = 2
TILE = 256
X, C, OUT, GRAD = 0, 1, 2, 3
GATE, UP, DOWN = 0, 1, 2
CROSS = (((1,), (1,)), ((), ()))
OUTER = (((0,), (0,)), ((), ()))


def layer_kernel(
    n, span,
    xs, cs, pick, weight, wg_in, wu_in, wd_in,
    output, grad_tokens, grad_down,
    xa, ca, out_rows, grad_rows, out_back, grad_back,
    wg, wu, wd, own, got, hidden, gg, gu,
    w_sem, send_sem, recv_sem, dp_send, dp_recv,
):
    me = lax.axis_index("expert")
    other = 1 - lax.axis_index("dp")
    rows = n * span
    feats = xs.shape[1]
    width = hidden.shape[1]
    sources = {X: xs, C: cs, OUT: out_rows, GRAD: grad_rows}
    targets = {X: xa, C: ca, OUT: out_back, GRAD: grad_back}

    loads = [
        pltpu.make_async_copy(src, dst, w_sem.at[i])
        for i, (src, dst) in enumerate(((wg_in, wg), (wu_in, wu), (wd_in, wd)))
    ]
    for load in loads:
        load.start()

    barrier = pltpu.get_barrier_semaphore()

    @pl.loop(1, n)
    def _(d):
        pl.semaphore_signal(barrier, inc=1, device_id={"expert": lax.rem(me + d, n)})

    pl.semaphore_signal(barrier, inc=1, device_id={"dp": other})
    pl.semaphore_wait(barrier, n)

    def block(piece, peer):
        return pl.ds(pl.multiple_of(piece * rows + peer * span, span), span)

    def piece_rows(piece):
        return pl.ds(piece * rows, rows)

    def remote(kind, piece, peer, landing):
        return pltpu.make_async_remote_copy(
            src_ref=sources[kind].at[block(piece, peer)],
            dst_ref=targets[kind].at[block(piece, landing)],
            send_sem=send_sem.at[kind * PIECES + piece, peer],
            recv_sem=recv_sem.at[kind * PIECES + piece, landing],
            device_id={"expert": peer},
        )

    def stay(kind, piece):
        return pltpu.make_async_copy(
            sources[kind].at[block(piece, me)],
            targets[kind].at[block(piece, me)],
            recv_sem.at[kind * PIECES + piece, me],
        )

    def send(kind, piece):
        @pl.loop(1, n)
        def _(d):
            remote(kind, piece, lax.rem(me + d, n), me).start()

        stay(kind, piece).start()

    def arrive(kind, piece):
        @pl.loop(1, n)
        def _(d):
            peer = lax.rem(me + d, n)
            remote(kind, piece, peer, peer).wait_recv()

        stay(kind, piece).wait()

    def partial(kind, piece):
        return pltpu.make_async_remote_copy(
            src_ref=own.at[kind, piece_rows(piece)],
            dst_ref=got.at[kind, piece_rows(piece)],
            send_sem=dp_send.at[kind, piece],
            recv_sem=dp_recv.at[kind, piece],
            device_id={"dp": other},
        )

    def total(kind, at):
        return own[kind, at, :].astype(jnp.float32) + got[kind, at, :].astype(jnp.float32)

    def columns(step):
        return pl.ds(pl.multiple_of(step * TILE, TILE), TILE)

    for piece in range(PIECES):
        send(X, piece)
    for piece in range(PIECES):
        send(C, piece)
    for load in loads:
        load.wait()

    def project(piece):
        arrive(X, piece)
        at = piece_rows(piece)
        for kind, matrix in ((GATE, wg), (UP, wu)):
            @pl.loop(0, width // TILE)
            def _(step):
                part = jnp.dot(
                    xa[at, :], matrix[:, columns(step)], preferred_element_type=jnp.float32
                )
                own[kind, at, columns(step)] = part.astype(jnp.bfloat16)

        partial(GATE, piece).start()
        partial(UP, piece).start()

    def forward(piece):
        partial(GATE, piece).wait_recv()
        partial(UP, piece).wait_recv()

        @pl.loop(0, rows // 32)
        def _(step):
            at = pl.ds(pl.multiple_of(piece * rows + step * 32, 32), 32)
            gate_pre = total(GATE, at)
            value = gate_pre * jax.nn.sigmoid(gate_pre) * total(UP, at)
            hidden[at, :] = value.astype(jnp.bfloat16)

        at = piece_rows(piece)

        @pl.loop(0, feats // TILE)
        def _(step):
            part = jnp.dot(
                hidden[at, :], wd[:, columns(step)], preferred_element_type=jnp.float32
            )
            out_rows[at, columns(step)] = part.astype(jnp.bfloat16)

        send(OUT, piece)

    def pull(piece):
        arrive(C, piece)
        at = piece_rows(piece)

        @pl.loop(0, width // TILE)
        def _(step):
            part = lax.dot_general(
                ca[at, :], wd[columns(step), :], CROSS, preferred_element_type=jnp.float32
            )
            own[DOWN, at, columns(step)] = part.astype(jnp.bfloat16)

        partial(DOWN, piece).start()

    def backward(piece):
        partial(DOWN, piece).wait_recv()

        @pl.loop(0, rows // 32)
        def _(step):
            at = pl.ds(pl.multiple_of(piece * rows + step * 32, 32), 32)
            here = pl.ds(pl.multiple_of(step * 32, 32), 32)
            gate_pre = total(GATE, at)
            up_pre = total(UP, at)
            grad_hidden = total(DOWN, at)
            sig = jax.nn.sigmoid(gate_pre)
            grad_gate = grad_hidden * up_pre * sig * (1.0 + gate_pre * (1.0 - sig))
            gg[here, :] = grad_gate.astype(jnp.bfloat16)
            gu[here, :] = (grad_hidden * (gate_pre * sig)).astype(jnp.bfloat16)

        @pl.loop(0, feats // TILE)
        def _(step):
            part = lax.dot_general(
                gg[...], wg[columns(step), :], CROSS, preferred_element_type=jnp.float32
            )
            part = part + lax.dot_general(
                gu[...], wu[columns(step), :], CROSS, preferred_element_type=jnp.float32
            )
            grad_rows[piece_rows(piece), columns(step)] = part.astype(jnp.bfloat16)

        send(GRAD, piece)

    project(0)
    project(1)
    forward(0)
    pull(0)
    forward(1)
    pull(1)
    backward(0)
    backward(1)

    @pl.loop(0, width // TILE)
    def _(step):
        @pl.loop(0, feats // TILE)
        def _(col):
            part = lax.dot_general(
                hidden[:, columns(step)], ca[:, columns(col)], OUTER,
                preferred_element_type=jnp.float32,
            )
            grad_down[columns(step), columns(col)] = part.astype(jnp.bfloat16)

    for piece in range(PIECES):
        arrive(OUT, piece)

    @pl.loop(0, feats // TILE)
    def _(step):
        scaled = (out_back[:, columns(step)].astype(jnp.float32) * weight[...]).astype(jnp.bfloat16)
        part = lax.dot_general(pick[...], scaled, OUTER, preferred_element_type=jnp.float32)
        output[:, columns(step)] = part.astype(jnp.bfloat16)

    for piece in range(PIECES):
        arrive(GRAD, piece)

    @pl.loop(0, feats // TILE)
    def _(step):
        part = lax.dot_general(
            pick[...], grad_back[:, columns(step)], OUTER, preferred_element_type=jnp.float32
        )
        grad_tokens[:, columns(step)] = part.astype(jnp.bfloat16)

    for kind in (GATE, UP, DOWN):
        for piece in range(PIECES):
            partial(kind, piece).wait_send()

    @pl.loop(1, n)
    def _(d):
        peer = lax.rem(me + d, n)
        for kind in (X, C, OUT, GRAD):
            for piece in range(PIECES):
                remote(kind, piece, peer, me).wait_send()


def fused(tokens, gate_of, placing, w_gate, w_up, w_down, grad_out):
    experts, capacity, tok_dev = placing.shape
    feats = tokens.shape[1]
    width = w_gate.shape[2]
    span = capacity // PIECES
    total = experts * capacity
    placing = placing.reshape(experts, PIECES, span, tok_dev).transpose(1, 0, 2, 3)
    pick = placing.astype(jnp.bfloat16).reshape(total, tok_dev)
    weight = jnp.sum(jnp.where(placing, gate_of[None, :, None, :], 0.0), axis=3).reshape(total, 1)
    xs = jnp.dot(pick, tokens, preferred_element_type=jnp.float32).astype(jnp.bfloat16)
    cs = jnp.dot(pick, grad_out, preferred_element_type=jnp.float32)
    cs = (weight * cs).astype(jnp.bfloat16)
    slab = pltpu.VMEM((total, feats), jnp.bfloat16)
    vmem = pl.BlockSpec(memory_space=pltpu.VMEM)
    anywhere = pl.BlockSpec(memory_space=pl.ANY)
    output, grad_tokens, grad_down = pl.pallas_call(
        functools.partial(layer_kernel, experts, span),
        out_shape=(
            jax.ShapeDtypeStruct((tok_dev, feats), jnp.bfloat16),
            jax.ShapeDtypeStruct((tok_dev, feats), jnp.bfloat16),
            jax.ShapeDtypeStruct((width, feats), jnp.bfloat16),
        ),
        in_specs=[vmem] * 4 + [anywhere] * 3,
        out_specs=(vmem, vmem, vmem),
        scratch_shapes=[slab] * 6
        + [
            pltpu.VMEM((feats, width), jnp.bfloat16),
            pltpu.VMEM((feats, width), jnp.bfloat16),
            pltpu.VMEM((width, feats), jnp.bfloat16),
            pltpu.VMEM((3, total, width), jnp.bfloat16),
            pltpu.VMEM((3, total, width), jnp.bfloat16),
            pltpu.VMEM((total, width), jnp.bfloat16),
            pltpu.VMEM((total // PIECES, width), jnp.bfloat16),
            pltpu.VMEM((total // PIECES, width), jnp.bfloat16),
            pltpu.SemaphoreType.DMA((3,)),
            pltpu.SemaphoreType.DMA((4 * PIECES, experts)),
            pltpu.SemaphoreType.DMA((4 * PIECES, experts)),
            pltpu.SemaphoreType.DMA((3, PIECES)),
            pltpu.SemaphoreType.DMA((3, PIECES)),
        ],
        compiler_params=pltpu.CompilerParams(collective_id=0, has_side_effects=True),
    )(xs, cs, pick, weight, w_gate[0], w_up[0], w_down[0])
    return output, grad_tokens, grad_down[None]


def local(tokens, expert_ids, gate_weight, w_gate, w_up, w_down, grad_out):
    tok_dev, fanout = expert_ids.shape
    feature_cols = tokens.shape[1]
    experts = lax.axis_size("expert")
    capacity = max(2, min(tok_dev, 2 * tok_dev * fanout // (4 * experts)))
    ids = jnp.arange(experts, dtype=jnp.int32)
    named = expert_ids[None, :, :] == ids[:, None, None]
    hot = jnp.any(named, axis=2)
    gate_of = jnp.sum(jnp.where(named, gate_weight[None, :, :], 0.0), axis=2)
    rows = jnp.arange(tok_dev, dtype=jnp.int32)
    earlier = (rows[:, None] < rows[None, :]).astype(jnp.bfloat16)
    before = jnp.dot(hot.astype(jnp.bfloat16), earlier, preferred_element_type=jnp.float32)
    slot_of = jnp.where(hot, before.astype(jnp.int32), -1)
    placing = slot_of[:, None, :] == jnp.arange(capacity, dtype=jnp.int32)[None, :, None]
    aligned = capacity % (16 * PIECES) == 0 and tok_dev % 128 == 0
    aligned = aligned and feature_cols % TILE == 0 and w_gate.shape[2] % TILE == 0
    if aligned and lax.axis_size("dp") == 2:
        return fused(tokens, gate_of, placing, w_gate, w_up, w_down, grad_out)
    select = placing.astype(jnp.bfloat16).reshape(experts * capacity, tok_dev)
    slot_gate = jnp.sum(jnp.where(placing, gate_of[:, None, :], 0.0), axis=2).reshape(experts * capacity)
    row_total = experts * capacity
    transposed = (((1,), (1,)), ((), ()))
    gate_mat = w_gate[0]
    up_mat = w_up[0]
    down_mat = w_down[0]

    pieces = 2
    span = capacity // pieces
    select_slots = select.reshape(experts, capacity, tok_dev)
    arrived = None
    gate_parts, up_parts, ready = [], [], []
    for piece in range(pieces):
        chosen = select_slots[:, piece * span : (piece + 1) * span].reshape(experts * span, tok_dev)
        x_slab = jnp.dot(chosen, tokens, preferred_element_type=jnp.float32).astype(jnp.bfloat16)
        arrived = exchange(x_slab.reshape(experts, span, feature_cols), arrived)
        x_rows = arrived.reshape(experts * span, feature_cols)
        gate_part = jnp.dot(x_rows, gate_mat, preferred_element_type=jnp.float32).astype(jnp.bfloat16)
        up_part = jnp.dot(x_rows, up_mat, preferred_element_type=jnp.float32).astype(jnp.bfloat16)
        gate_parts.append(dp_sum(gate_part))
        up_parts.append(dp_sum(up_part))
        ready.append((gate_parts[-1], up_part))

    cot_rows = jnp.dot(select, grad_out, preferred_element_type=jnp.float32)
    c_slab = (slot_gate[:, None] * cot_rows).astype(jnp.bfloat16)
    c_arrived = exchange(c_slab.reshape(experts, capacity, feature_cols), (arrived, ready[0]))
    c_rows = c_arrived.reshape(row_total, feature_cols)
    hidden_part = lax.dot_general(c_rows, down_mat, transposed, preferred_element_type=jnp.float32)

    def joined(parts):
        parts = [part.reshape(experts, span, part.shape[1]) for part in parts]
        return jnp.concatenate(parts, axis=1).reshape(row_total, parts[0].shape[2])

    gate_pre, up_pre = joined(gate_parts), joined(up_parts)
    hidden = (jax.nn.silu(gate_pre) * up_pre).astype(jnp.bfloat16)
    out_rows = jnp.dot(hidden, down_mat, preferred_element_type=jnp.float32).astype(jnp.bfloat16)
    back_out = exchange(out_rows.reshape(experts, capacity, feature_cols), c_arrived)

    grad_hidden = dp_sum(hidden_part)
    sig = jax.nn.sigmoid(gate_pre)
    grad_gate = (grad_hidden * up_pre * sig * (1.0 + gate_pre * (1.0 - sig))).astype(jnp.bfloat16)
    grad_up = (grad_hidden * jax.nn.silu(gate_pre)).astype(jnp.bfloat16)
    grad_rows = lax.dot_general(grad_gate, gate_mat, transposed, preferred_element_type=jnp.float32)
    grad_rows = grad_rows + lax.dot_general(
        grad_up, up_mat, transposed, preferred_element_type=jnp.float32
    )
    grad_rows = grad_rows.astype(jnp.bfloat16).reshape(experts, capacity, feature_cols)
    back_grads = exchange(grad_rows, back_out)
    down_grad = lax.dot_general(
        hidden, c_rows, (((0,), (0,)), ((), ())), preferred_element_type=jnp.float32
    ).astype(jnp.bfloat16)

    scaled = back_out.reshape(row_total, feature_cols).astype(jnp.float32) * slot_gate[:, None]
    output = jnp.dot(select.T, scaled.astype(jnp.bfloat16), preferred_element_type=jnp.float32)
    output = output.astype(jnp.bfloat16)
    grad_flat = back_grads.reshape(row_total, feature_cols)
    grad_tokens = jnp.dot(select.T, grad_flat, preferred_element_type=jnp.float32).astype(
        jnp.bfloat16
    )
    return (output, grad_tokens, down_grad.reshape(1, down_grad.shape[0], feature_cols))


def solution(mesh):
    return jax.shard_map(
        local,
        mesh=mesh,
        in_specs=(
            P("expert", "dp"),
            P("expert", None),
            P("expert", None),
            P("expert", "dp", None),
            P("expert", "dp", None),
            P("expert", None, "dp"),
            P("expert", "dp"),
        ),
        out_specs=(P("expert", "dp"), P("expert", "dp"), P("expert", None, "dp")),
        check_vma=False,
    )
```
